32 devices in a mesh: lat: 4 (over x, core), lon: 8 (over z, y).
Axes of the slice: x: 2, y: 2, z: 4, core: 2. Of those that a mesh axis runs over, the one named last changes fastest.
Arguments:
- atmosphere_inputs: bfloat16 [9, 512, 1024], P(None, 'lat', 'lon'), may hold values from -6 to 6
- thermal_anomaly: float32 [64, 131072], P(None, ('lat', 'lon')), may hold values from -6 to 6
- mixing_rates: float32 [64, 131072], P(None, ('lat', 'lon')), may hold values from 0.1 to 10
- adjacency_table: int32 [6, 131072], P(None, ('lat', 'lon')), may hold values from 0 to 4351
- lateral_spread_factor: float32 [6, 131072], P(None, ('lat', 'lon')), may hold values from 0.02 to 0.15
- sent_vertices: int32 [256, 32], P(('lat', 'lon')), may hold values from 0 to 4095
- corner_parallel: int32 [4, 131072], P(None, ('lat', 'lon')), may hold values from 0 to 127, as said below
- corner_longitude: int32 [4, 131072], P(None, ('lat', 'lon')), may hold values from 0 to 1023, as said below
- corner_share: float32 [4, 131072], P(None, ('lat', 'lon')), as said below
- exchange_factor: float32 [9], replicated, may hold values from -3 to 3
- sensitivity_vector: float32 [64, 131072], P(None, ('lat', 'lon')), may hold values from -6 to 6
Outputs:
- updated_warmth: float32 [64, 131072], P(None, ('lat', 'lon'))
- temp_grad: float32 [64, 131072], P(None, ('lat', 'lon'))
- forcing_grad: float32 [9, 512, 1024], P(None, 'lat', 'lon')
The draws below stay inside these ranges and needn't reach their ends.
Inputs may be any that keep to these rules, and one draw needn't show every extreme that they name: `adjacency_table`: entries below 4096 are the partition's own nodes; entry 4096 + c * 32 + h is the h-th halo node received from the c-th partition of its group. `sent_vertices`: row p * 8 + c lists local nodes of partition p sent to the c-th partition of its group. `corner_parallel`: the four stencil points of a node are rows r, r + 1, r, r + 1 of its latitude band. `corner_longitude`: the four stencil points of a node are columns c, c, c + 1, c + 1 taken modulo 1024; for a partition of lon index b all of them lie in the 256 columns from b * 128 - 128 / 2 on, taken modulo 1024, and both ends of that window are named by some node of every partition. `corner_share`: products (1 - u)(1 - v), u (1 - v), (1 - u) v, u v of the node's row fraction u and column fraction v.
All inputs are finite; a program needn't handle non-finite values.
Results may differ from the reference program's by a relative error of at most 0.00055.
Values may be sent and summed in bfloat16 or wider, within the bound.
A program may use at most 128 MiB of HBM per device.

```python
import math
import jax
import jax.numpy as jnp
from jax import lax

FIELDS = 9
TILE = 128
DEPTH_LAYERS = 64
NEIGH = 6
NODES_DEV = 4096
HALO = 32
NLAT = 512
NLON = 1024
MESH_VERTICES = 131072
N_LAT = 4
N_LON = 8
DEVICES = 32


def stencil_base(key):
    key_col, key_row = jax.random.split(jax.random.fold_in(key, 7))
    node = jnp.arange(MESH_VERTICES).astype(jnp.int32)
    local = node % NODES_DEV
    owner = node // NODES_DEV
    offset = jax.random.randint(key_col, (MESH_VERTICES,), 0, 2 * TILE - 1).astype(jnp.int32)
    offset = jnp.where(local == 0, 0, jnp.where(local == 1, 2 * TILE - 2, offset))
    base_col = (owner % N_LON * TILE - TILE // 2 + offset) % NLON
    base_row = jax.random.randint(key_row, (MESH_VERTICES,), 0, TILE - 1).astype(jnp.int32)
    base_row = jnp.where(local == 0, 0, jnp.where(local == 1, TILE - 2, base_row))
    return (base_row.astype(jnp.int32), base_col.astype(jnp.int32))


def draw_corner_parallel(key, part):
    base_row, base_col = stencil_base(key)
    return jnp.stack([base_row, base_row + 1, base_row, base_row + 1], 0).astype(jnp.int32)


def draw_corner_longitude(key, part):
    base_row, base_col = stencil_base(key)
    next_col = (base_col + 1) % NLON
    return jnp.stack([base_col, base_col, next_col, next_col], 0).astype(jnp.int32)


def draw_corner_share(key, part):
    key_u, key_v = jax.random.split(jax.random.fold_in(key, 11))
    frac_u = jax.random.uniform(key_u, (MESH_VERTICES,), jnp.float32)
    frac_v = jax.random.uniform(key_v, (MESH_VERTICES,), jnp.float32)
    return jnp.stack([(1.0 - frac_u) * (1.0 - frac_v), frac_u * (1.0 - frac_v), (1.0 - frac_u) * frac_v, frac_u * frac_v], 0).astype(jnp.float32)


def set_ends(values, stream_key, least, top_value):
    longest = values.shape.index(max(values.shape))
    spots = []
    for shift in (0, 1):
        where = [jax.random.randint(jax.random.fold_in(stream_key, axis), (), 0, length) for axis, length in enumerate(values.shape)]
        where[longest] = (where[longest] + shift) % values.shape[longest]
        spots.append(tuple(where))
    return values.at[spots[0]].set(least).at[spots[1]].set(top_value)


def block_scale(own_key, dims, cuts, smallest, top_value):
    factor_of = 1.0
    for axis_at, parts in cuts:
        draws = jax.random.uniform(jax.random.fold_in(jax.random.fold_in(own_key, 6), axis_at), (parts,), jnp.float32, smallest / len(cuts), top_value / len(cuts))
        factor_of = factor_of * jnp.repeat(jnp.exp(draws), dims[axis_at] // parts).reshape((-1,) + (1,) * (len(dims) - 1 - axis_at))
    return factor_of


def centred(rng, dims, deviation, most, pieces=(), dtype=jnp.bfloat16):
    gain = block_scale(rng, dims, pieces, -0.22, 0.18) if pieces else 1.0
    array = jax.random.normal(rng, dims, jnp.float32) * deviation * gain
    return jnp.minimum(jnp.maximum(array, -most), most).astype(dtype)


def setup_inputs(seed: int = 0) -> dict:
    keys = jax.random.split(jax.random.key(seed), 12)
    return {
        "atmosphere_inputs": centred(keys[0], (FIELDS, NLAT, NLON), 1.0, 6.0, ((1, 4), (2, 8))),
        "thermal_anomaly": centred(keys[1], (DEPTH_LAYERS, MESH_VERTICES), 1.0, 6.0, ((1, 32),), jnp.float32),
        "mixing_rates": jnp.clip(jnp.exp(math.log(10.0) - 4.6051702 * jax.random.uniform(keys[2], (DEPTH_LAYERS, MESH_VERTICES), jnp.float32) ** block_scale(keys[2], (DEPTH_LAYERS, MESH_VERTICES), ((1, 32),), -0.2, 0.2)), 0.1, 10.0),
        "adjacency_table": set_ends(jax.random.randint(keys[3], (NEIGH, MESH_VERTICES), 0, NODES_DEV + N_LON * HALO), jax.random.fold_in(keys[3], 1), 0, (NODES_DEV + N_LON * HALO) - 1).astype(jnp.int32),
        "lateral_spread_factor": jnp.clip(0.02 + 0.13000001 * jax.random.uniform(keys[4], (NEIGH, MESH_VERTICES), jnp.float32) ** block_scale(keys[4], (NEIGH, MESH_VERTICES), ((1, 32),), -0.2, 0.2), 0.02, 0.15),
        "sent_vertices": set_ends(jax.random.randint(keys[5], (DEVICES * N_LON, HALO), 0, NODES_DEV), jax.random.fold_in(keys[5], 1), 0, NODES_DEV - 1).astype(jnp.int32),
        "corner_parallel": draw_corner_parallel(jax.random.fold_in(keys[11], 71), 0),
        "corner_longitude": draw_corner_longitude(jax.random.fold_in(keys[11], 71), 0),
        "corner_share": draw_corner_share(jax.random.fold_in(keys[11], 71), 0),
        "exchange_factor": centred(keys[9], (FIELDS,), 0.5, 3.0, (), jnp.float32),
        "sensitivity_vector": centred(keys[10], (DEPTH_LAYERS, MESH_VERTICES), 1.0, 6.0, ((1, 32),), jnp.float32),
    }


def column_solve(mixing_rates, source_vector):
    zero_row = jnp.zeros_like(mixing_rates[:1])
    prev_k = jnp.concatenate([zero_row, mixing_rates[:-1]], 0)
    above_k = jnp.concatenate([-mixing_rates[:-1], zero_row], 0)
    diagonal = 1.0 + prev_k + mixing_rates

    def sweep_down(carry, level_items):
        c_prev, d_prev = carry
        below_row, diag_row, above_row, rhs_row = level_items
        pivot = diag_row - below_row * c_prev
        c_next = above_row / pivot
        d_next = (rhs_row - below_row * d_prev) / pivot
        return ((c_next, d_next), (c_next, d_next))
    start = (jnp.zeros_like(mixing_rates[0]), jnp.zeros_like(mixing_rates[0]))
    _, (c_all, d_all) = lax.scan(sweep_down, start, (-prev_k, diagonal, above_k, source_vector))

    def sweep_up(x_next, level_items):
        c_row, d_row = level_items
        x_row = d_row - c_row * x_next
        return (x_row, x_row)
    _, solved = lax.scan(sweep_up, jnp.zeros_like(mixing_rates[0]), (c_all, d_all), reverse=True)
    return solved

def inner_portion(parallel_band, thermal_anomaly, extended_vertices, mixing_rates, adjacency_table, lateral_spread_factor, corner_position, corner_share, exchange_factor, sensitivity_vector):
    fields = parallel_band.shape[0]
    vertex_total = thermal_anomaly.shape[1]
    points = jnp.take(parallel_band, corner_position.reshape(-1), axis=1).astype(jnp.float32).reshape(fields, 4, vertex_total)
    driven_profile = lax.optimization_barrier(jnp.sum(points * corner_share[None], 1))
    breeze_drive = jnp.sqrt(driven_profile[0] * driven_profile[0] + driven_profile[1] * driven_profile[1] + 1.0)
    boundary_transfer = lax.optimization_barrier(jnp.sum(exchange_factor[:, None] * driven_profile, 0)) + 0.1 * breeze_drive * (driven_profile[2] - thermal_anomaly[0])
    gathered_entries = jnp.take(extended_vertices, adjacency_table, axis=1)
    source_vector = thermal_anomaly + lax.optimization_barrier(jnp.sum(lateral_spread_factor[None] * (gathered_entries - thermal_anomaly[:, None, :]), 1))
    source_vector = source_vector.at[0].add(boundary_transfer)
    updated_warmth = column_solve(mixing_rates, source_vector)
    adjoint = column_solve(mixing_rates, sensitivity_vector)
    surface = adjoint[0]
    spread = lateral_spread_factor[None] * adjoint[:, None, :]
    ext_grad = jnp.zeros_like(extended_vertices).at[:, adjacency_table].add(spread)
    temp_grad = adjoint * (1.0 - lax.optimization_barrier(jnp.sum(lateral_spread_factor, 0)))[None] + ext_grad[:, :vertex_total]
    temp_grad = temp_grad.at[0].add(-0.1 * surface * breeze_drive)
    excess_quantity = 0.1 * (driven_profile[2] - thermal_anomaly[0]) / breeze_drive
    node_grad = surface[None] * exchange_factor[:, None]
    node_grad = node_grad.at[0].add(surface * excess_quantity * driven_profile[0])
    node_grad = node_grad.at[1].add(surface * excess_quantity * driven_profile[1])
    node_grad = node_grad.at[2].add(surface * 0.1 * breeze_drive)
    entries_list = (node_grad[:, None, :] * corner_share[None]).reshape(fields, 4 * vertex_total)
    return (updated_warmth, temp_grad, ext_grad[:, vertex_total:], entries_list)

def reference(atmosphere_inputs, thermal_anomaly, mixing_rates, adjacency_table, lateral_spread_factor, sent_vertices, corner_parallel, corner_longitude, corner_share, exchange_factor, sensitivity_vector):

    def split_pieces(whole):
        return whole.reshape(whole.shape[0], DEVICES, NODES_DEV).transpose(1, 0, 2)
    corner_position = (corner_parallel * NLON + corner_longitude).astype(jnp.int32)
    thermal_portion = split_pieces(thermal_anomaly)
    sequences = sent_vertices.reshape(DEVICES, N_LON, HALO)
    departing_border = jax.vmap(lambda quantity_layer, matrix_lines: jnp.take(quantity_layer, matrix_lines, axis=1))(thermal_portion, sequences)
    received_border = departing_border.reshape(N_LAT, N_LON, DEPTH_LAYERS, N_LON, HALO).transpose(0, 3, 2, 1, 4).reshape(DEVICES, DEPTH_LAYERS, N_LON * HALO)
    extended_vertices = jnp.concatenate([thermal_portion, received_border], 2)
    bands = atmosphere_inputs.reshape(FIELDS, N_LAT, TILE, NLON).transpose(1, 0, 2, 3).reshape(N_LAT, FIELDS, TILE * NLON)
    processor_labels = jnp.arange(DEVICES).astype(jnp.int32)

    def single_processor(items):
        ident, temp_one, ext_one, kv_one, nbr_one, coef_one, idx_one, wgt_one, cot_one = items
        parallel_band = bands[ident // N_LON]
        return inner_portion(parallel_band, temp_one, ext_one, kv_one, nbr_one, coef_one, idx_one, wgt_one, exchange_factor, cot_one)
    updated_warmth, owned_derivative, border_derivative, entries_list = lax.map(single_processor, (processor_labels, thermal_portion, extended_vertices, split_pieces(mixing_rates), split_pieces(adjacency_table), split_pieces(lateral_spread_factor), split_pieces(corner_position), split_pieces(corner_share), split_pieces(sensitivity_vector)))
    back = border_derivative.reshape(N_LAT, N_LON, DEPTH_LAYERS, N_LON, HALO).transpose(0, 3, 2, 1, 4).reshape(DEVICES, DEPTH_LAYERS, N_LON, HALO)
    temp_grad = jax.vmap(lambda grad_one, matrix_lines, back_one: grad_one.at[:, matrix_lines].add(back_one))(owned_derivative, sequences, back)
    flat_index = split_pieces(corner_position).reshape(N_LAT, N_LON * 4 * NODES_DEV)
    band_values = entries_list.reshape(N_LAT, N_LON, FIELDS, 4 * NODES_DEV).transpose(0, 2, 1, 3).reshape(N_LAT, FIELDS, N_LON * 4 * NODES_DEV)
    band_grad = jax.vmap(lambda index_row, value_rows: jnp.zeros((FIELDS, TILE * NLON), jnp.float32).at[:, index_row].add(value_rows))(flat_index, band_values)
    forcing_grad = band_grad.reshape(N_LAT, FIELDS, TILE, NLON).transpose(1, 0, 2, 3).reshape(FIELDS, NLAT, NLON)

    def join(per_device):
        return per_device.transpose(1, 0, 2).reshape(DEPTH_LAYERS, MESH_VERTICES)
    return (join(updated_warmth), join(temp_grad), forcing_grad)
```

```python
import functools

import jax
import jax.numpy as jnp
from jax import lax
from jax.experimental import pallas as pl
from jax.experimental.pallas import tpu as pltpu
from jax.sharding import PartitionSpec as P

F32 = jnp.float32
BF16 = jnp.bfloat16
VMEM_BYTES = 56 * 1024 * 1024
LANES = 128
SLOT_ROWS = 256
NODE_TILE = 512


def whole(count):
    return [pl.BlockSpec(memory_space=pltpu.VMEM)] * count


def halves(value):
    high = lax.reduce_precision(value, 8, 7)
    return high.astype(BF16), (value - high).astype(BF16)


def adjoint_kernel(mix_ref, rhs_ref, x_ref, gain_ref, scale_ref, carry_ref):
    layers = mix_ref.shape[0]
    zero = jnp.zeros(mix_ref.shape[1:], F32)

    def down(level, state):
        mix_prev, gain_prev, d_prev = state
        mix = mix_ref[level]
        scale = 1.0 / (1.0 + mix + mix_prev * (1.0 - gain_prev))
        gain = mix * scale
        carry = mix_prev * scale
        d_next = rhs_ref[level] * scale + carry * d_prev
        gain_ref[level] = gain
        scale_ref[level] = scale
        carry_ref[level] = carry
        x_ref[level] = d_next
        return mix, gain, d_next

    lax.fori_loop(0, layers, down, (zero, zero, zero), unroll=4)

    def up(step, x_next):
        level = layers - 1 - step
        x_here = x_ref[level] + gain_ref[level] * x_next
        x_ref[level] = x_here
        return x_here

    lax.fori_loop(0, layers, up, zero, unroll=8)


def forward_kernel(rhs_ref, gain_ref, scale_ref, carry_ref, x_ref):
    layers = rhs_ref.shape[0]
    zero = jnp.zeros(rhs_ref.shape[1:], F32)

    def down(level, d_prev):
        d_next = rhs_ref[level] * scale_ref[level] + carry_ref[level] * d_prev
        x_ref[level] = d_next
        return d_next

    lax.fori_loop(0, layers, down, zero, unroll=8)

    def up(step, x_next):
        level = layers - 1 - step
        x_here = x_ref[level] + gain_ref[level] * x_next
        x_ref[level] = x_here
        return x_here

    lax.fori_loop(0, layers, up, zero, unroll=8)


def lateral_kernel(adj_ref, coef_ref, ext_ref, adjoint_ref, spread_ref, grad_ref, merged_ref):
    step = pl.program_id(0)
    slots, nodes = adj_ref.shape
    layers = grad_ref.shape[0]

    @pl.when(step == 0)
    def _():
        for k in range(slots):
            same = coef_ref[k : k + 1, :]
            for m in range(slots):
                if m != k:
                    equal = adj_ref[k : k + 1, :] == adj_ref[m : m + 1, :]
                    same = same + jnp.where(equal, coef_ref[m : m + 1, :], 0.0)
            merged_ref[k : k + 1, :] = same

    row = lax.broadcasted_iota(jnp.int32, (SLOT_ROWS, NODE_TILE), 0).astype(F32).astype(BF16)
    ext = ext_ref[...]
    total = jnp.zeros((2 * layers, SLOT_ROWS), F32)
    fine = jnp.zeros((layers, SLOT_ROWS), F32)
    for tile in range(nodes // NODE_TILE):
        cols = pl.ds(tile * NODE_TILE, NODE_TILE)
        local = (adj_ref[:, cols] - step * SLOT_ROWS).astype(F32).astype(BF16)
        share, rest = halves(merged_ref[:, cols])
        weights = jnp.zeros((SLOT_ROWS, NODE_TILE), BF16)
        small = jnp.zeros((SLOT_ROWS, NODE_TILE), BF16)
        for k in range(slots):
            here = row == local[k : k + 1, :]
            weights = jnp.where(here, share[k : k + 1, :], weights)
            small = jnp.where(here, rest[k : k + 1, :], small)
        part = jnp.dot(ext, weights, preferred_element_type=F32)
        part = part[:layers] + part[layers:]
        part += jnp.dot(ext[:layers], small, preferred_element_type=F32)

        @pl.when(step == 0)
        def _(part=part, cols=cols):
            spread_ref[:, cols] = part

        @pl.when(step > 0)
        def _(part=part, cols=cols):
            spread_ref[:, cols] += part

        contract = (((1,), (1,)), ((), ()))
        total += lax.dot_general(
            adjoint_ref[:, cols], weights, contract, preferred_element_type=F32
        )
        fine += lax.dot_general(
            adjoint_ref[:layers, cols], small, contract, preferred_element_type=F32
        )
    grad_ref[...] = total[:layers] + total[layers:] + fine


def forcing_kernel(
    start_ref,
    factor_ref,
    window_ref,
    row_ref,
    col_ref,
    share_ref,
    surface_ref,
    thermal_ref,
    flux_ref,
    corr_ref,
    grad_ref,
    *,
    band_width,
):
    fields, tile_rows, window_cols = grad_ref.shape
    tile = row_ref.shape[1]

    @pl.when(pl.program_id(0) == 0)
    def _():
        grad_ref[...] = jnp.zeros_like(grad_ref)

    share = share_ref[...]
    row_low = share[0:1] + share[2:3]
    row_high = share[1:2] + share[3:4]
    col_low = share[0:1] + share[1:2]
    col_high = share[2:3] + share[3:4]
    base_row = row_ref[0:1, :]
    base_col = col_ref[0:1, :] - start_ref[0]
    base_col = jnp.where(base_col < 0, base_col + band_width, base_col)
    base_col = jnp.where(base_col >= band_width, base_col - band_width, base_col)
    row_at = lax.broadcasted_iota(jnp.int32, (tile_rows, tile), 0)
    col_at = lax.broadcasted_iota(jnp.int32, (window_cols, tile), 0)
    rows = jnp.where(
        row_at == base_row, row_low, jnp.where(row_at == base_row + 1, row_high, 0.0)
    )
    cols = jnp.where(
        col_at == base_col, col_low, jnp.where(col_at == base_col + 1, col_high, 0.0)
    )
    cols_hi, cols_lo = halves(cols)
    forced = []
    for f in range(fields):
        field = window_ref[f]
        mixed = jnp.dot(field, cols_hi, preferred_element_type=F32)
        mixed = mixed + jnp.dot(field, cols_lo, preferred_element_type=F32)
        forced.append(jnp.sum(mixed * rows, axis=0, keepdims=True))
    wind = jnp.sqrt(forced[0] * forced[0] + forced[1] * forced[1] + 1.0)
    excess = forced[2] - thermal_ref[...]
    flux = 0.1 * wind * excess
    for f in range(fields):
        flux = flux + factor_ref[f] * forced[f]
    flux_ref[...] = flux
    surface = surface_ref[...]
    corr_ref[...] = -0.1 * surface * wind
    quotient = surface * (0.1 * excess / wind)
    contract = (((1,), (1,)), ((), ()))
    for f in range(fields):
        node_grad = surface * factor_ref[f]
        if f < 2:
            node_grad = node_grad + quotient * forced[f]
        if f == 2:
            node_grad = node_grad + 0.1 * surface * wind
        left_hi, left_lo = halves(node_grad * rows)
        dot = functools.partial(
            lax.dot_general, dimension_numbers=contract, preferred_element_type=F32
        )
        grad_ref[f] += dot(left_hi, cols_hi) + dot(left_lo, cols_hi) + dot(left_hi, cols_lo)


def cost(flops, moved):
    return pl.CostEstimate(flops=flops, bytes_accessed=moved, transcendentals=0)


def per_device(
    atmosphere_inputs,
    thermal_anomaly,
    mixing_rates,
    adjacency_table,
    lateral_spread_factor,
    sent_vertices,
    corner_parallel,
    corner_longitude,
    corner_share,
    exchange_factor,
    sensitivity_vector,
):
    layers, nodes = thermal_anomaly.shape
    fields, tile_rows, tile_cols = atmosphere_inputs.shape
    half = tile_cols // 2
    columns = lax.axis_size("lon")
    halo = columns * sent_vertices.shape[1]
    slots = adjacency_table.shape[0]
    band_width = tile_cols * columns
    window_cols = 2 * tile_cols
    extended = nodes + halo
    params = pltpu.CompilerParams(vmem_limit_bytes=VMEM_BYTES)
    upward = [(i, (i + 1) % columns) for i in range(columns)]
    downward = [((i + 1) % columns, i) for i in range(columns)]
    start = (lax.axis_index("lon") * tile_cols - half).astype(jnp.int32).reshape(1)

    from_left = lax.ppermute(atmosphere_inputs[:, :, tile_cols - half :], "lon", upward)
    from_right = lax.ppermute(atmosphere_inputs[:, :, :half], "lon", downward)

    node_at = lax.broadcasted_iota(jnp.int32, (halo, nodes), 1)
    chosen = (sent_vertices.reshape(halo, 1) == node_at).astype(BF16)
    departing = lax.dot_general(
        chosen,
        thermal_anomaly.astype(BF16),
        (((1,), (1,)), ((), ())),
        preferred_element_type=F32,
    ).astype(BF16)
    received = lax.all_to_all(
        departing.reshape(columns, halo // columns, layers),
        "lon",
        split_axis=0,
        concat_axis=0,
        tiled=True,
    ).reshape(halo, layers)

    dense = (layers, nodes // LANES, LANES)
    block = jax.ShapeDtypeStruct(dense, F32)
    adjoint3, gain, scale, carry = pl.pallas_call(
        adjoint_kernel,
        out_shape=(block,) * 4,
        in_specs=whole(2),
        out_specs=tuple(whole(4)),
        compiler_params=params,
        cost_estimate=cost(layers * nodes * 20, layers * nodes * 24),
        name="adjoint_solve",
    )(mixing_rates.reshape(dense), sensitivity_vector.reshape(dense))
    adjoint = adjoint3.reshape(layers, nodes)
    surface = adjoint3[0].reshape(1, nodes)

    window = jnp.concatenate([from_left, atmosphere_inputs, from_right], 2)
    line = pl.BlockSpec((1, NODE_TILE), lambda i: (0, i))
    four = pl.BlockSpec((4, NODE_TILE), lambda i: (0, i))
    flux, corr, window_grad = pl.pallas_call(
        functools.partial(forcing_kernel, band_width=band_width),
        grid=(nodes // NODE_TILE,),
        out_shape=(
            jax.ShapeDtypeStruct((1, nodes), F32),
            jax.ShapeDtypeStruct((1, nodes), F32),
            jax.ShapeDtypeStruct((fields, tile_rows, window_cols), F32),
        ),
        in_specs=[
            pl.BlockSpec(memory_space=pltpu.SMEM),
            pl.BlockSpec(memory_space=pltpu.SMEM),
            pl.BlockSpec((fields, tile_rows, window_cols), lambda i: (0, 0, 0)),
            four,
            four,
            four,
            line,
            line,
        ],
        out_specs=(
            line,
            line,
            pl.BlockSpec((fields, tile_rows, window_cols), lambda i: (0, 0, 0)),
        ),
        compiler_params=params,
        cost_estimate=cost(10 * fields * tile_rows * window_cols * nodes, 4000000),
        name="forcing",
    )(
        start,
        exchange_factor,
        window,
        corner_parallel,
        corner_longitude,
        corner_share,
        surface,
        thermal_anomaly[0:1],
    )
    rim_from_left = lax.ppermute(window_grad[:, :, window_cols - half :], "lon", upward)
    rim_from_right = lax.ppermute(window_grad[:, :, :half], "lon", downward)

    thermal_hi, thermal_lo = halves(thermal_anomaly)
    received = received.T
    ext = jnp.concatenate(
        [
            jnp.concatenate([thermal_hi, received], 1),
            jnp.concatenate([thermal_lo, jnp.zeros_like(received)], 1),
        ],
        0,
    )
    spread, grad = pl.pallas_call(
        lateral_kernel,
        grid=(extended // SLOT_ROWS,),
        out_shape=(
            jax.ShapeDtypeStruct((layers, nodes), F32),
            jax.ShapeDtypeStruct((layers, extended), F32),
        ),
        in_specs=[
            pl.BlockSpec((slots, nodes), lambda i: (0, 0)),
            pl.BlockSpec((slots, nodes), lambda i: (0, 0)),
            pl.BlockSpec((2 * layers, SLOT_ROWS), lambda i: (0, i)),
            pl.BlockSpec((2 * layers, nodes), lambda i: (0, 0)),
        ],
        out_specs=(
            pl.BlockSpec((layers, nodes), lambda i: (0, 0)),
            pl.BlockSpec((layers, SLOT_ROWS), lambda i: (0, i)),
        ),
        scratch_shapes=[pltpu.VMEM((slots, nodes), F32)],
        compiler_params=params,
        cost_estimate=cost(8 * layers * nodes * extended, 8000000),
        name="lateral",
    )(
        adjacency_table,
        lateral_spread_factor,
        ext,
        jnp.concatenate(halves(adjoint), 0),
    )
    halo_grad = grad[:, nodes:].astype(BF16).T
    back = lax.all_to_all(
        halo_grad.reshape(columns, halo // columns, layers),
        "lon",
        split_axis=0,
        concat_axis=0,
        tiled=True,
    ).reshape(halo, layers)

    keep = 1.0 - jnp.sum(lateral_spread_factor, 0, keepdims=True)
    top = lax.broadcasted_iota(jnp.int32, (layers, nodes), 0) == 0
    rhs = thermal_anomaly * keep + spread + jnp.where(top, flux, 0.0)
    updated = pl.pallas_call(
        forward_kernel,
        out_shape=block,
        in_specs=whole(4),
        out_specs=pl.BlockSpec(memory_space=pltpu.VMEM),
        compiler_params=params,
        cost_estimate=cost(layers * nodes * 6, layers * nodes * 20),
        name="forward_solve",
    )(rhs.reshape(dense), gain, scale, carry)
    updated_warmth = updated.reshape(layers, nodes)

    returned = lax.dot_general(
        back, chosen, (((0,), (0,)), ((), ())), preferred_element_type=F32
    )
    temp_grad = adjoint * keep + grad[:, :nodes] + jnp.where(top, corr, 0.0) + returned
    forcing_grad = window_grad[:, :, half : half + tile_cols] + jnp.concatenate(
        [rim_from_left, rim_from_right], 2
    )
    return (updated_warmth, temp_grad, forcing_grad)


def solution(mesh):
    nodes = P(None, ("lat", "lon"))
    placed = (
        P(None, "lat", "lon"),
        nodes,
        nodes,
        nodes,
        nodes,
        P(("lat", "lon"), None),
        nodes,
        nodes,
        nodes,
        P(),
        nodes,
    )
    return jax.shard_map(
        per_device,
        mesh=mesh,
        in_specs=placed,
        out_specs=(nodes, nodes, P(None, "lat", "lon")),
        check_vma=False,
    )
```

```python
import functools

import jax
import jax.numpy as jnp
from jax import lax
from jax.experimental import pallas as pl
from jax.experimental.pallas import tpu as pltpu
from jax.sharding import PartitionSpec as P

F32 = jnp.float32
BF16 = jnp.bfloat16
VMEM_BYTES = 56 * 1024 * 1024
LANES = 128
SLOT_ROWS = 256
NODE_TILE = 256
FORCE_TILE = 512


def whole(count):
    return [pl.BlockSpec(memory_space=pltpu.VMEM)] * count


def halves(value):
    high = value.astype(BF16)
    return high, (value - high.astype(F32)).astype(BF16)


def spread_levels(source_ref, dense_ref):
    layers = dense_ref.shape[0]
    for level in range(0, layers, 8):
        dense_ref[level : level + 8] = source_ref[level : level + 8, :].reshape(
            (8,) + dense_ref.shape[1:]
        )


def sweep_up(x_ref, gain_ref, zero):
    layers = x_ref.shape[0]

    def up(step, x_next):
        level = layers - 1 - step
        x_here = x_ref[level] + gain_ref[level] * x_next
        x_ref[level] = x_here
        return x_here

    lax.fori_loop(0, layers, up, zero, unroll=8)


def adjoint_kernel(
    mix_ref, rhs_ref, parts_ref, surface_ref, gain_ref, scale_ref, carry_ref, mix3_ref, x_ref
):
    layers, nodes = mix_ref.shape
    zero = jnp.zeros(x_ref.shape[1:], F32)
    spread_levels(mix_ref, mix3_ref)
    spread_levels(rhs_ref, x_ref)

    def down(level, state):
        mix_prev, gain_prev, d_prev = state
        mix = mix3_ref[level]
        scale = 1.0 / (1.0 + mix + mix_prev * (1.0 - gain_prev))
        gain = mix * scale
        carry = mix_prev * scale
        d_next = x_ref[level] * scale + carry * d_prev
        gain_ref[level] = gain
        scale_ref[level] = scale
        carry_ref[level] = carry
        x_ref[level] = d_next
        return mix, gain, d_next

    lax.fori_loop(0, layers, down, (zero, zero, zero), unroll=4)
    sweep_up(x_ref, gain_ref, zero)
    for level in range(0, layers, 16):
        flat = x_ref[level : level + 16].reshape(16, nodes)
        if level == 0:
            surface_ref[...] = flat[0:1]
        high, low = halves(flat)
        parts_ref[level : level + 16, :] = high
        parts_ref[layers + level : layers + level + 16, :] = low


def forward_kernel(rhs_ref, flux_ref, gain_ref, scale_ref, carry_ref, out_ref, x_ref):
    layers, nodes = rhs_ref.shape
    zero = jnp.zeros(x_ref.shape[1:], F32)
    spread_levels(rhs_ref, x_ref)
    x_ref[0] = x_ref[0] + flux_ref[...].reshape(x_ref.shape[1:])

    def down(level, d_prev):
        d_next = x_ref[level] * scale_ref[level] + carry_ref[level] * d_prev
        x_ref[level] = d_next
        return d_next

    lax.fori_loop(0, layers, down, zero, unroll=8)
    sweep_up(x_ref, gain_ref, zero)
    for level in range(0, layers, 8):
        out_ref[level : level + 8, :] = x_ref[level : level + 8].reshape(8, nodes)


def lateral_kernel(
    adj_ref, coef_ref, thermal_ref, received_ref, parts_ref, rhs_ref, own_ref, halo_ref, merged_ref
):
    step = pl.program_id(0)
    slots, nodes = adj_ref.shape
    layers = rhs_ref.shape[0]
    own_steps = nodes // SLOT_ROWS
    contract = (((1,), (1,)), ((), ()))

    @pl.when(step == 0)
    def _():
        for k in range(slots):
            same = coef_ref[k : k + 1, :]
            for m in range(slots):
                if m != k:
                    equal = adj_ref[k : k + 1, :] == adj_ref[m : m + 1, :]
                    same = same + jnp.where(equal, coef_ref[m : m + 1, :], 0.0)
            merged_ref[k : k + 1, :] = same
        keep = 1.0 - jnp.sum(coef_ref[...], axis=0, keepdims=True)
        rhs_ref[...] = thermal_ref[...] * keep

    here = pl.ds(pl.multiple_of(jnp.minimum(step, own_steps - 1) * SLOT_ROWS, SLOT_ROWS), SLOT_ROWS)
    high, low = halves(thermal_ref[:, here])
    is_own = step < own_steps
    high = jnp.where(is_own, high, received_ref[...])
    low = jnp.where(is_own, low, jnp.zeros_like(low))
    ext = jnp.concatenate([high, low], 0)
    row = lax.broadcasted_iota(jnp.int32, (SLOT_ROWS, NODE_TILE), 0).astype(F32).astype(BF16)
    total = jnp.zeros((2 * layers, SLOT_ROWS), F32)
    fine = jnp.zeros((layers, SLOT_ROWS), F32)
    for tile in range(nodes // NODE_TILE):
        cols = pl.ds(tile * NODE_TILE, NODE_TILE)
        local = (adj_ref[:, cols] - step * SLOT_ROWS).astype(F32).astype(BF16)
        share, rest = halves(merged_ref[:, cols])
        weights = jnp.zeros((SLOT_ROWS, NODE_TILE), BF16)
        small = jnp.zeros((SLOT_ROWS, NODE_TILE), BF16)
        for k in range(slots):
            match = row == local[k : k + 1, :]
            weights = jnp.where(match, share[k : k + 1, :], weights)
            small = jnp.where(match, rest[k : k + 1, :], small)
        part = jnp.dot(ext, weights, preferred_element_type=F32)
        part = part[:layers] + part[layers:]
        rhs_ref[:, cols] += part + jnp.dot(ext[:layers], small, preferred_element_type=F32)
        total += lax.dot_general(
            parts_ref[:, cols], weights, contract, preferred_element_type=F32
        )
        fine += lax.dot_general(
            parts_ref[:layers, cols], small, contract, preferred_element_type=F32
        )
    grad = total[:layers] + total[layers:] + fine

    @pl.when(is_own)
    def _():
        keep = 1.0 - jnp.sum(coef_ref[:, here], axis=0, keepdims=True)
        whole_x = parts_ref[:layers, here].astype(F32) + parts_ref[layers:, here].astype(F32)
        own_ref[...] = whole_x * keep + grad

    @pl.when(jnp.logical_not(is_own))
    def _():
        halo_ref[...] = grad.T.astype(BF16)


def forcing_kernel(
    start_ref,
    factor_ref,
    window_ref,
    row_ref,
    col_ref,
    share_ref,
    surface_ref,
    thermal_ref,
    flux_ref,
    corr_ref,
    own_ref,
    left_ref,
    right_ref,
    grad_ref,
    *,
    band_width,
):
    fields, tile_rows, window_cols = grad_ref.shape
    half = left_ref.shape[2]
    tile = row_ref.shape[1]

    @pl.when(pl.program_id(0) == 0)
    def _():
        grad_ref[...] = jnp.zeros_like(grad_ref)

    share = share_ref[...]
    row_low = share[0:1] + share[2:3]
    row_high = share[1:2] + share[3:4]
    col_low = share[0:1] + share[1:2]
    col_high = share[2:3] + share[3:4]
    base_row = row_ref[0:1, :]
    base_col = col_ref[0:1, :] - start_ref[0]
    base_col = jnp.where(base_col < 0, base_col + band_width, base_col)
    base_col = jnp.where(base_col >= band_width, base_col - band_width, base_col)
    row_at = lax.broadcasted_iota(jnp.int32, (tile_rows, tile), 0)
    col_at = lax.broadcasted_iota(jnp.int32, (window_cols, tile), 0)
    rows = jnp.where(
        row_at == base_row, row_low, jnp.where(row_at == base_row + 1, row_high, 0.0)
    )
    cols = jnp.where(
        col_at == base_col, col_low, jnp.where(col_at == base_col + 1, col_high, 0.0)
    )
    cols_hi, cols_lo = halves(cols)
    window = window_ref[...].reshape(fields * tile_rows, window_cols)
    mixed = jnp.dot(window, cols_hi, preferred_element_type=F32)
    mixed = mixed + jnp.dot(window, cols_lo, preferred_element_type=F32)
    forced = [
        jnp.sum(mixed[f * tile_rows : (f + 1) * tile_rows] * rows, axis=0, keepdims=True)
        for f in range(fields)
    ]
    wind = jnp.sqrt(forced[0] * forced[0] + forced[1] * forced[1] + 1.0)
    excess = forced[2] - thermal_ref[...]
    flux = 0.1 * wind * excess
    for f in range(fields):
        flux = flux + factor_ref[f] * forced[f]
    flux_ref[...] = flux
    surface = surface_ref[...]
    corr_ref[...] = -0.1 * surface * wind
    quotient = surface * (0.1 * excess / wind)
    dot = functools.partial(
        lax.dot_general,
        dimension_numbers=(((1,), (1,)), ((), ())),
        preferred_element_type=F32,
    )
    lefts = []
    for f in range(fields):
        node_grad = surface * factor_ref[f]
        if f < 2:
            node_grad = node_grad + quotient * forced[f]
        if f == 2:
            node_grad = node_grad + 0.1 * surface * wind
        lefts.append(halves(node_grad * rows))
    left_hi = jnp.concatenate([high for high, _ in lefts], 0)
    left_lo = jnp.concatenate([low for _, low in lefts], 0)
    grad = dot(left_hi, cols_hi) + dot(left_lo, cols_hi) + dot(left_hi, cols_lo)
    grad_ref[...] += grad.reshape(fields, tile_rows, window_cols)

    @pl.when(pl.program_id(0) == pl.num_programs(0) - 1)
    def _():
        for f in range(fields):
            grad = grad_ref[f]
            left_ref[f] = grad[:, :half]
            right_ref[f] = grad[:, window_cols - half :]
            own_ref[f] = grad[:, half : window_cols - half]


def cost(flops, moved):
    return pl.CostEstimate(flops=flops, bytes_accessed=moved, transcendentals=0)


def per_device(
    atmosphere_inputs,
    thermal_anomaly,
    mixing_rates,
    adjacency_table,
    lateral_spread_factor,
    sent_vertices,
    corner_parallel,
    corner_longitude,
    corner_share,
    exchange_factor,
    sensitivity_vector,
):
    layers, nodes = thermal_anomaly.shape
    fields, tile_rows, tile_cols = atmosphere_inputs.shape
    half = tile_cols // 2
    columns = lax.axis_size("lon")
    halo = columns * sent_vertices.shape[1]
    slots = adjacency_table.shape[0]
    band_width = tile_cols * columns
    window_cols = 2 * tile_cols
    extended = nodes + halo
    params = pltpu.CompilerParams(vmem_limit_bytes=VMEM_BYTES)
    upward = [(i, (i + 1) % columns) for i in range(columns)]
    downward = [((i + 1) % columns, i) for i in range(columns)]
    start = (lax.axis_index("lon") * tile_cols - half).astype(jnp.int32).reshape(1)

    from_left = lax.ppermute(atmosphere_inputs[:, :, tile_cols - half :], "lon", upward)
    from_right = lax.ppermute(atmosphere_inputs[:, :, :half], "lon", downward)

    node_at = lax.broadcasted_iota(jnp.int32, (halo, nodes), 1)
    chosen = (sent_vertices.reshape(halo, 1) == node_at).astype(BF16)
    departing = lax.dot_general(
        chosen,
        thermal_anomaly.astype(BF16),
        (((1,), (1,)), ((), ())),
        preferred_element_type=F32,
    ).astype(BF16)
    received = lax.all_to_all(
        departing.reshape(columns, halo // columns, layers),
        "lon",
        split_axis=0,
        concat_axis=0,
        tiled=True,
    ).reshape(halo, layers)

    dense = (layers, nodes // LANES, LANES)
    block = jax.ShapeDtypeStruct(dense, F32)
    parts, surface, gain, scale, carry = pl.pallas_call(
        adjoint_kernel,
        out_shape=(
            jax.ShapeDtypeStruct((2 * layers, nodes), BF16),
            jax.ShapeDtypeStruct((1, nodes), F32),
            block,
            block,
            block,
        ),
        in_specs=whole(2),
        out_specs=tuple(whole(5)),
        scratch_shapes=[pltpu.VMEM(dense, F32), pltpu.VMEM(dense, F32)],
        compiler_params=params,
        cost_estimate=cost(layers * nodes * 20, layers * nodes * 24),
        name="adjoint_solve",
    )(mixing_rates, sensitivity_vector)

    own_steps = nodes // SLOT_ROWS
    rhs, own_grad, halo_grad = pl.pallas_call(
        lateral_kernel,
        grid=(extended // SLOT_ROWS,),
        out_shape=(
            jax.ShapeDtypeStruct((layers, nodes), F32),
            jax.ShapeDtypeStruct((layers, nodes), F32),
            jax.ShapeDtypeStruct((halo, layers), BF16),
        ),
        in_specs=[
            pl.BlockSpec((slots, nodes), lambda i: (0, 0)),
            pl.BlockSpec((slots, nodes), lambda i: (0, 0)),
            pl.BlockSpec((layers, nodes), lambda i: (0, 0)),
            pl.BlockSpec((layers, SLOT_ROWS), lambda i: (0, jnp.maximum(i - own_steps, 0))),
            pl.BlockSpec((2 * layers, nodes), lambda i: (0, 0)),
        ],
        out_specs=(
            pl.BlockSpec((layers, nodes), lambda i: (0, 0)),
            pl.BlockSpec((layers, SLOT_ROWS), lambda i: (0, jnp.minimum(i, own_steps - 1))),
            pl.BlockSpec((SLOT_ROWS, layers), lambda i: (jnp.maximum(i - own_steps, 0), 0)),
        ),
        scratch_shapes=[pltpu.VMEM((slots, nodes), F32)],
        compiler_params=params,
        cost_estimate=cost(8 * layers * nodes * extended, 8000000),
        name="lateral",
    )(
        adjacency_table,
        lateral_spread_factor,
        thermal_anomaly,
        received.T,
        parts,
    )
    back = lax.all_to_all(
        halo_grad.reshape(columns, halo // columns, layers),
        "lon",
        split_axis=0,
        concat_axis=0,
        tiled=True,
    ).reshape(halo, layers)

    window = jnp.concatenate([from_left, atmosphere_inputs, from_right], 2)
    line = pl.BlockSpec((1, FORCE_TILE), lambda i: (0, i))
    four = pl.BlockSpec((4, FORCE_TILE), lambda i: (0, i))

    def all_of(width):
        return pl.BlockSpec((fields, tile_rows, width), lambda i: (0, 0, 0))

    def grid_shape(width):
        return jax.ShapeDtypeStruct((fields, tile_rows, width), F32)

    flux, corr, own_forcing, left_rim, right_rim = pl.pallas_call(
        functools.partial(forcing_kernel, band_width=band_width),
        grid=(nodes // FORCE_TILE,),
        out_shape=(
            jax.ShapeDtypeStruct((1, nodes), F32),
            jax.ShapeDtypeStruct((1, nodes), F32),
            grid_shape(tile_cols),
            grid_shape(half),
            grid_shape(half),
        ),
        in_specs=[
            pl.BlockSpec(memory_space=pltpu.SMEM),
            pl.BlockSpec(memory_space=pltpu.SMEM),
            all_of(window_cols),
            four,
            four,
            four,
            line,
            line,
        ],
        out_specs=(line, line, all_of(tile_cols), all_of(half), all_of(half)),
        scratch_shapes=[pltpu.VMEM((fields, tile_rows, window_cols), F32)],
        compiler_params=params,
        cost_estimate=cost(8 * fields * tile_rows * window_cols * nodes, 4000000),
        name="forcing",
    )(
        start,
        exchange_factor,
        window,
        corner_parallel,
        corner_longitude,
        corner_share,
        surface,
        thermal_anomaly[0:1],
    )
    rim_from_left = lax.ppermute(right_rim, "lon", upward)
    rim_from_right = lax.ppermute(left_rim, "lon", downward)

    updated_warmth = pl.pallas_call(
        forward_kernel,
        out_shape=jax.ShapeDtypeStruct((layers, nodes), F32),
        in_specs=whole(5),
        out_specs=pl.BlockSpec(memory_space=pltpu.VMEM),
        scratch_shapes=[pltpu.VMEM(dense, F32)],
        compiler_params=params,
        cost_estimate=cost(layers * nodes * 6, layers * nodes * 20),
        name="forward_solve",
    )(rhs, flux, gain, scale, carry)

    returned = lax.dot_general(
        back, chosen, (((0,), (0,)), ((), ())), preferred_element_type=F32
    )
    top = lax.broadcasted_iota(jnp.int32, (layers, nodes), 0) == 0
    temp_grad = own_grad + jnp.where(top, corr, 0.0) + returned
    forcing_grad = own_forcing + jnp.concatenate([rim_from_left, rim_from_right], 2)
    return (updated_warmth, temp_grad, forcing_grad)


def solution(mesh):
    nodes = P(None, ("lat", "lon"))
    placed = (
        P(None, "lat", "lon"),
        nodes,
        nodes,
        nodes,
        nodes,
        P(("lat", "lon"), None),
        nodes,
        nodes,
        nodes,
        P(),
        nodes,
    )
    return jax.shard_map(
        per_device,
        mesh=mesh,
        in_specs=placed,
        out_specs=(nodes, nodes, P(None, "lat", "lon")),
        check_vma=False,
    )
```

```python
import functools

import jax
import jax.numpy as jnp
from jax import lax
from jax.experimental import pallas as pl
from jax.experimental.pallas import tpu as pltpu
from jax.sharding import PartitionSpec as P

F32 = jnp.float32
BF16 = jnp.bfloat16
VMEM_BYTES = 56 * 1024 * 1024
LANES = 128
SLOT_ROWS = 256
NODE_TILE = 256
FORCE_TILE = 512


def whole(count):
    return [pl.BlockSpec(memory_space=pltpu.VMEM)] * count


def halves(value):
    high = value.astype(BF16)
    return high, (value - high.astype(F32)).astype(BF16)


def spread_levels(source_ref, dense_ref):
    layers = dense_ref.shape[0]
    for level in range(0, layers, 8):
        dense_ref[level : level + 8] = source_ref[level : level + 8, :].reshape(
            (8,) + dense_ref.shape[1:]
        )


def sweep_up(x_ref, gain_ref, zero):
    layers = x_ref.shape[0]

    def up(step, x_next):
        level = layers - 1 - step
        x_here = x_ref[level] + gain_ref[level] * x_next
        x_ref[level] = x_here
        return x_here

    lax.fori_loop(0, layers, up, zero, unroll=8)


def best_scale(values, count):
    trial = lax.broadcasted_iota(jnp.int32, (count, values[0].shape[1]), 0).astype(F32)
    trial = 1.0 + trial * (1.0 / count)
    inverse = 1.0 / trial
    miss = jnp.zeros_like(trial)
    for value in values:
        gap = (value * inverse).astype(BF16).astype(F32) * trial - value
        miss = miss + gap * gap
    least = jnp.min(miss, axis=0, keepdims=True)
    return jnp.max(jnp.where(miss == least, trial, 1.0), axis=0, keepdims=True)


def adjoint_kernel(
    mix_ref, rhs_ref, parts_ref, surface_ref, gain_ref, scale_ref, carry_ref, mix3_ref, x_ref
):
    layers, nodes = mix_ref.shape
    zero = jnp.zeros(x_ref.shape[1:], F32)
    spread_levels(mix_ref, mix3_ref)
    spread_levels(rhs_ref, x_ref)

    def down(level, state):
        mix_prev, gain_prev, d_prev = state
        mix = mix3_ref[level]
        scale = 1.0 / (1.0 + mix + mix_prev * (1.0 - gain_prev))
        gain = mix * scale
        carry = mix_prev * scale
        d_next = x_ref[level] * scale + carry * d_prev
        gain_ref[level] = gain
        scale_ref[level] = scale
        carry_ref[level] = carry
        x_ref[level] = d_next
        return mix, gain, d_next

    lax.fori_loop(0, layers, down, (zero, zero, zero), unroll=4)
    sweep_up(x_ref, gain_ref, zero)
    for level in range(0, layers, 16):
        flat = x_ref[level : level + 16].reshape(16, nodes)
        if level == 0:
            surface_ref[...] = flat[0:1]
        high, low = halves(flat)
        parts_ref[level : level + 16, :] = high
        parts_ref[layers + level : layers + level + 16, :] = low


def forward_kernel(rhs_ref, flux_ref, gain_ref, scale_ref, carry_ref, out_ref, x_ref):
    layers, nodes = rhs_ref.shape
    zero = jnp.zeros(x_ref.shape[1:], F32)
    spread_levels(rhs_ref, x_ref)
    x_ref[0] = x_ref[0] + flux_ref[...].reshape(x_ref.shape[1:])

    def down(level, d_prev):
        d_next = x_ref[level] * scale_ref[level] + carry_ref[level] * d_prev
        x_ref[level] = d_next
        return d_next

    lax.fori_loop(0, layers, down, zero, unroll=8)
    sweep_up(x_ref, gain_ref, zero)
    for level in range(0, layers, 8):
        out_ref[level : level + 8, :] = x_ref[level : level + 8].reshape(8, nodes)


def lateral_kernel(
    adj_ref,
    coef_ref,
    thermal_ref,
    received_ref,
    parts_ref,
    rhs_ref,
    own_ref,
    halo_ref,
    merged_ref,
    scale_ref,
    scaled_ref,
):
    step = pl.program_id(0)
    slots, nodes = adj_ref.shape
    layers = rhs_ref.shape[0]
    own_steps = nodes // SLOT_ROWS
    contract = (((1,), (1,)), ((), ()))

    @pl.when(step == 0)
    def _():
        for k in range(slots):
            same = coef_ref[k : k + 1, :]
            for m in range(slots):
                if m != k:
                    equal = adj_ref[k : k + 1, :] == adj_ref[m : m + 1, :]
                    same = same + jnp.where(equal, coef_ref[m : m + 1, :], 0.0)
            merged_ref[k : k + 1, :] = same
        keep = 1.0 - jnp.sum(coef_ref[...], axis=0, keepdims=True)
        rhs_ref[...] = thermal_ref[...] * keep
        for tile in range(nodes // NODE_TILE):
            cols = pl.ds(tile * NODE_TILE, NODE_TILE)
            merged = [merged_ref[k : k + 1, cols] for k in range(slots)]
            scale = best_scale(merged, 64)
            scale_ref[:, cols] = scale
            merged_ref[:, cols] = merged_ref[:, cols] / scale
            x = parts_ref[:layers, cols].astype(F32) + parts_ref[layers:, cols].astype(F32)
            x_high, x_low = halves(x * scale)
            scaled_ref[:layers, cols] = x_high
            scaled_ref[layers:, cols] = x_low

    here = pl.ds(pl.multiple_of(jnp.minimum(step, own_steps - 1) * SLOT_ROWS, SLOT_ROWS), SLOT_ROWS)
    high, low = halves(thermal_ref[:, here])
    is_own = step < own_steps
    high = jnp.where(is_own, high, received_ref[...])
    low = jnp.where(is_own, low, jnp.zeros_like(low))
    ext = jnp.concatenate([high, low], 0)
    row = lax.broadcasted_iota(jnp.int32, (SLOT_ROWS, NODE_TILE), 0).astype(F32).astype(BF16)
    total = jnp.zeros((2 * layers, SLOT_ROWS), F32)
    for tile in range(nodes // NODE_TILE):
        cols = pl.ds(tile * NODE_TILE, NODE_TILE)
        local = (adj_ref[:, cols] - step * SLOT_ROWS).astype(F32).astype(BF16)
        share = merged_ref[:, cols].astype(BF16)
        weights = jnp.zeros((SLOT_ROWS, NODE_TILE), BF16)
        for k in range(slots):
            weights = jnp.where(row == local[k : k + 1, :], share[k : k + 1, :], weights)
        part = jnp.dot(ext, weights, preferred_element_type=F32)
        rhs_ref[:, cols] += (part[:layers] + part[layers:]) * scale_ref[:, cols]
        total += lax.dot_general(
            scaled_ref[:, cols], weights, contract, preferred_element_type=F32
        )
    grad = total[:layers] + total[layers:]

    @pl.when(is_own)
    def _():
        keep = 1.0 - jnp.sum(coef_ref[:, here], axis=0, keepdims=True)
        whole_x = parts_ref[:layers, here].astype(F32) + parts_ref[layers:, here].astype(F32)
        own_ref[...] = whole_x * keep + grad

    @pl.when(jnp.logical_not(is_own))
    def _():
        halo_ref[...] = grad.T.astype(BF16)


def forcing_kernel(
    start_ref,
    factor_ref,
    window_ref,
    row_ref,
    col_ref,
    share_ref,
    surface_ref,
    thermal_ref,
    flux_ref,
    corr_ref,
    own_ref,
    left_ref,
    right_ref,
    grad_ref,
    *,
    band_width,
):
    fields, tile_rows, window_cols = grad_ref.shape
    half = left_ref.shape[2]
    tile = row_ref.shape[1]

    @pl.when(pl.program_id(0) == 0)
    def _():
        grad_ref[...] = jnp.zeros_like(grad_ref)

    share = share_ref[...]
    row_low = share[0:1] + share[2:3]
    row_high = share[1:2] + share[3:4]
    col_low = share[0:1] + share[1:2]
    col_high = share[2:3] + share[3:4]
    scale = best_scale([col_low, col_high], 64)
    col_low = col_low / scale
    col_high = col_high / scale
    base_row = row_ref[0:1, :]
    base_col = col_ref[0:1, :] - start_ref[0]
    base_col = jnp.where(base_col < 0, base_col + band_width, base_col)
    base_col = jnp.where(base_col >= band_width, base_col - band_width, base_col)
    row_at = lax.broadcasted_iota(jnp.int32, (tile_rows, tile), 0)
    col_at = lax.broadcasted_iota(jnp.int32, (window_cols, tile), 0)
    rows = jnp.where(
        row_at == base_row, row_low, jnp.where(row_at == base_row + 1, row_high, 0.0)
    )
    cols = jnp.where(
        col_at == base_col, col_low, jnp.where(col_at == base_col + 1, col_high, 0.0)
    )
    cols = cols.astype(BF16)
    window = window_ref[...].reshape(fields * tile_rows, window_cols)
    rows = rows * scale
    mixed = jnp.dot(window, cols, preferred_element_type=F32)
    forced = [
        jnp.sum(mixed[f * tile_rows : (f + 1) * tile_rows] * rows, axis=0, keepdims=True)
        for f in range(fields)
    ]
    wind = jnp.sqrt(forced[0] * forced[0] + forced[1] * forced[1] + 1.0)
    excess = forced[2] - thermal_ref[...]
    flux = 0.1 * wind * excess
    for f in range(fields):
        flux = flux + factor_ref[f] * forced[f]
    flux_ref[...] = flux
    surface = surface_ref[...]
    corr_ref[...] = -0.1 * surface * wind
    quotient = surface * (0.1 * excess / wind)
    dot = functools.partial(
        lax.dot_general,
        dimension_numbers=(((1,), (1,)), ((), ())),
        preferred_element_type=F32,
    )
    lefts = []
    for f in range(fields):
        node_grad = surface * factor_ref[f]
        if f < 2:
            node_grad = node_grad + quotient * forced[f]
        if f == 2:
            node_grad = node_grad + 0.1 * surface * wind
        lefts.append(halves(node_grad * rows))
    left_hi = jnp.concatenate([high for high, _ in lefts], 0)
    left_lo = jnp.concatenate([low for _, low in lefts], 0)
    grad = dot(left_hi, cols) + dot(left_lo, cols)
    grad_ref[...] += grad.reshape(fields, tile_rows, window_cols)

    @pl.when(pl.program_id(0) == pl.num_programs(0) - 1)
    def _():
        for f in range(fields):
            grad = grad_ref[f]
            left_ref[f] = grad[:, :half]
            right_ref[f] = grad[:, window_cols - half :]
            own_ref[f] = grad[:, half : window_cols - half]


def cost(flops, moved):
    return pl.CostEstimate(flops=flops, bytes_accessed=moved, transcendentals=0)


def per_device(
    atmosphere_inputs,
    thermal_anomaly,
    mixing_rates,
    adjacency_table,
    lateral_spread_factor,
    sent_vertices,
    corner_parallel,
    corner_longitude,
    corner_share,
    exchange_factor,
    sensitivity_vector,
):
    layers, nodes = thermal_anomaly.shape
    fields, tile_rows, tile_cols = atmosphere_inputs.shape
    half = tile_cols // 2
    columns = lax.axis_size("lon")
    halo = columns * sent_vertices.shape[1]
    slots = adjacency_table.shape[0]
    band_width = tile_cols * columns
    window_cols = 2 * tile_cols
    extended = nodes + halo
    params = pltpu.CompilerParams(vmem_limit_bytes=VMEM_BYTES)
    upward = [(i, (i + 1) % columns) for i in range(columns)]
    downward = [((i + 1) % columns, i) for i in range(columns)]
    start = (lax.axis_index("lon") * tile_cols - half).astype(jnp.int32).reshape(1)

    from_left = lax.ppermute(atmosphere_inputs[:, :, tile_cols - half :], "lon", upward)
    from_right = lax.ppermute(atmosphere_inputs[:, :, :half], "lon", downward)

    node_at = lax.broadcasted_iota(jnp.int32, (halo, nodes), 1)
    chosen = (sent_vertices.reshape(halo, 1) == node_at).astype(BF16)
    departing = lax.dot_general(
        chosen,
        thermal_anomaly.astype(BF16),
        (((1,), (1,)), ((), ())),
        preferred_element_type=F32,
    ).astype(BF16)
    received = lax.all_to_all(
        departing.reshape(columns, halo // columns, layers),
        "lon",
        split_axis=0,
        concat_axis=0,
        tiled=True,
    ).reshape(halo, layers)

    dense = (layers, nodes // LANES, LANES)
    block = jax.ShapeDtypeStruct(dense, F32)
    parts, surface, gain, scale, carry = pl.pallas_call(
        adjoint_kernel,
        out_shape=(
            jax.ShapeDtypeStruct((2 * layers, nodes), BF16),
            jax.ShapeDtypeStruct((1, nodes), F32),
            block,
            block,
            block,
        ),
        in_specs=whole(2),
        out_specs=tuple(whole(5)),
        scratch_shapes=[pltpu.VMEM(dense, F32), pltpu.VMEM(dense, F32)],
        compiler_params=params,
        cost_estimate=cost(layers * nodes * 20, layers * nodes * 24),
        name="adjoint_solve",
    )(mixing_rates, sensitivity_vector)

    own_steps = nodes // SLOT_ROWS
    rhs, own_grad, halo_grad = pl.pallas_call(
        lateral_kernel,
        grid=(extended // SLOT_ROWS,),
        out_shape=(
            jax.ShapeDtypeStruct((layers, nodes), F32),
            jax.ShapeDtypeStruct((layers, nodes), F32),
            jax.ShapeDtypeStruct((halo, layers), BF16),
        ),
        in_specs=[
            pl.BlockSpec((slots, nodes), lambda i: (0, 0)),
            pl.BlockSpec((slots, nodes), lambda i: (0, 0)),
            pl.BlockSpec((layers, nodes), lambda i: (0, 0)),
            pl.BlockSpec((layers, SLOT_ROWS), lambda i: (0, jnp.maximum(i - own_steps, 0))),
            pl.BlockSpec((2 * layers, nodes), lambda i: (0, 0)),
        ],
        out_specs=(
            pl.BlockSpec((layers, nodes), lambda i: (0, 0)),
            pl.BlockSpec((layers, SLOT_ROWS), lambda i: (0, jnp.minimum(i, own_steps - 1))),
            pl.BlockSpec((SLOT_ROWS, layers), lambda i: (jnp.maximum(i - own_steps, 0), 0)),
        ),
        scratch_shapes=[
            pltpu.VMEM((slots, nodes), F32),
            pltpu.VMEM((1, nodes), F32),
            pltpu.VMEM((2 * layers, nodes), BF16),
        ],
        compiler_params=params,
        cost_estimate=cost(8 * layers * nodes * extended, 8000000),
        name="lateral",
    )(
        adjacency_table,
        lateral_spread_factor,
        thermal_anomaly,
        received.T,
        parts,
    )
    back = lax.all_to_all(
        halo_grad.reshape(columns, halo // columns, layers),
        "lon",
        split_axis=0,
        concat_axis=0,
        tiled=True,
    ).reshape(halo, layers)

    window = jnp.concatenate([from_left, atmosphere_inputs, from_right], 2)
    line = pl.BlockSpec((1, FORCE_TILE), lambda i: (0, i))
    four = pl.BlockSpec((4, FORCE_TILE), lambda i: (0, i))

    def all_of(width):
        return pl.BlockSpec((fields, tile_rows, width), lambda i: (0, 0, 0))

    def grid_shape(width):
        return jax.ShapeDtypeStruct((fields, tile_rows, width), F32)

    flux, corr, own_forcing, left_rim, right_rim = pl.pallas_call(
        functools.partial(forcing_kernel, band_width=band_width),
        grid=(nodes // FORCE_TILE,),
        out_shape=(
            jax.ShapeDtypeStruct((1, nodes), F32),
            jax.ShapeDtypeStruct((1, nodes), F32),
            grid_shape(tile_cols),
            grid_shape(half),
            grid_shape(half),
        ),
        in_specs=[
            pl.BlockSpec(memory_space=pltpu.SMEM),
            pl.BlockSpec(memory_space=pltpu.SMEM),
            all_of(window_cols),
            four,
            four,
            four,
            line,
            line,
        ],
        out_specs=(line, line, all_of(tile_cols), all_of(half), all_of(half)),
        scratch_shapes=[pltpu.VMEM((fields, tile_rows, window_cols), F32)],
        compiler_params=params,
        cost_estimate=cost(8 * fields * tile_rows * window_cols * nodes, 4000000),
        name="forcing",
    )(
        start,
        exchange_factor,
        window,
        corner_parallel,
        corner_longitude,
        corner_share,
        surface,
        thermal_anomaly[0:1],
    )
    rim_from_left = lax.ppermute(right_rim, "lon", upward)
    rim_from_right = lax.ppermute(left_rim, "lon", downward)

    updated_warmth = pl.pallas_call(
        forward_kernel,
        out_shape=jax.ShapeDtypeStruct((layers, nodes), F32),
        in_specs=whole(5),
        out_specs=pl.BlockSpec(memory_space=pltpu.VMEM),
        scratch_shapes=[pltpu.VMEM(dense, F32)],
        compiler_params=params,
        cost_estimate=cost(layers * nodes * 6, layers * nodes * 20),
        name="forward_solve",
    )(rhs, flux, gain, scale, carry)

    returned = lax.dot_general(
        back, chosen, (((0,), (0,)), ((), ())), preferred_element_type=F32
    )
    top = lax.broadcasted_iota(jnp.int32, (layers, nodes), 0) == 0
    temp_grad = own_grad + jnp.where(top, corr, 0.0) + returned
    forcing_grad = own_forcing + jnp.concatenate([rim_from_left, rim_from_right], 2)
    return (updated_warmth, temp_grad, forcing_grad)


def solution(mesh):
    nodes = P(None, ("lat", "lon"))
    placed = (
        P(None, "lat", "lon"),
        nodes,
        nodes,
        nodes,
        nodes,
        P(("lat", "lon"), None),
        nodes,
        nodes,
        nodes,
        P(),
        nodes,
    )
    return jax.shard_map(
        per_device,
        mesh=mesh,
        in_specs=placed,
        out_specs=(nodes, nodes, P(None, "lat", "lon")),
        check_vma=False,
    )
```

```python
import functools

import jax
import jax.numpy as jnp
from jax import lax
from jax.experimental import pallas as pl
from jax.experimental.pallas import tpu as pltpu
from jax.sharding import PartitionSpec as P

F32 = jnp.float32
BF16 = jnp.bfloat16
VMEM_BYTES = 56 * 1024 * 1024
LANES = 128
SLOT_ROWS = 256
NODE_TILE = 256
FORCE_TILE = 512


def whole(count):
    return [pl.BlockSpec(memory_space=pltpu.VMEM)] * count


def halves(value):
    high = value.astype(BF16)
    return high, (value - high.astype(F32)).astype(BF16)


def spread_levels(source_ref, dense_ref):
    layers = dense_ref.shape[0]
    for level in range(0, layers, 8):
        dense_ref[level : level + 8] = source_ref[level : level + 8, :].reshape(
            (8,) + dense_ref.shape[1:]
        )


def sweep_up(x_ref, gain_ref, zero):
    layers = x_ref.shape[0]

    def up(step, x_next):
        level = layers - 1 - step
        x_here = x_ref[level] + gain_ref[level] * x_next
        x_ref[level] = x_here
        return x_here

    lax.fori_loop(0, layers, up, zero, unroll=8)


def best_scale(values, count):
    trial = lax.broadcasted_iota(jnp.int32, (count, values[0].shape[1]), 0).astype(F32)
    trial = 1.0 + trial * (1.0 / count)
    inverse = 1.0 / trial
    miss = jnp.zeros_like(trial)
    for value in values:
        gap = (value * inverse).astype(BF16).astype(F32) * trial - value
        miss = miss + gap * gap
    least = jnp.min(miss, axis=0, keepdims=True)
    return jnp.max(jnp.where(miss == least, trial, 1.0), axis=0, keepdims=True)


def adjoint_kernel(
    mix_ref, rhs_ref, parts_ref, surface_ref, gain_ref, scale_ref, carry_ref, mix3_ref, x_ref
):
    layers, nodes = mix_ref.shape
    zero = jnp.zeros(x_ref.shape[1:], F32)
    spread_levels(mix_ref, mix3_ref)
    spread_levels(rhs_ref, x_ref)

    def down(level, state):
        mix_prev, gain_prev, d_prev = state
        mix = mix3_ref[level]
        scale = 1.0 / (1.0 + mix + mix_prev * (1.0 - gain_prev))
        gain = mix * scale
        carry = mix_prev * scale
        d_next = x_ref[level] * scale + carry * d_prev
        gain_ref[level] = gain
        scale_ref[level] = scale
        carry_ref[level] = carry
        x_ref[level] = d_next
        return mix, gain, d_next

    lax.fori_loop(0, layers, down, (zero, zero, zero), unroll=4)
    sweep_up(x_ref, gain_ref, zero)
    for level in range(0, layers, 16):
        flat = x_ref[level : level + 16].reshape(16, nodes)
        if level == 0:
            surface_ref[...] = flat[0:1]
        high, low = halves(flat)
        parts_ref[level : level + 16, :] = high
        parts_ref[layers + level : layers + level + 16, :] = low


def forward_kernel(rhs_ref, flux_ref, gain_ref, scale_ref, carry_ref, out_ref, x_ref):
    layers, nodes = rhs_ref.shape
    zero = jnp.zeros(x_ref.shape[1:], F32)
    spread_levels(rhs_ref, x_ref)
    x_ref[0] = x_ref[0] + flux_ref[...].reshape(x_ref.shape[1:])

    def down(level, d_prev):
        d_next = x_ref[level] * scale_ref[level] + carry_ref[level] * d_prev
        x_ref[level] = d_next
        return d_next

    lax.fori_loop(0, layers, down, zero, unroll=8)
    sweep_up(x_ref, gain_ref, zero)
    for level in range(0, layers, 8):
        out_ref[level : level + 8, :] = x_ref[level : level + 8].reshape(8, nodes)


def lateral_kernel(
    adj_ref,
    coef_ref,
    thermal_ref,
    received_ref,
    parts_ref,
    rhs_ref,
    own_ref,
    halo_ref,
    merged_ref,
    scale_ref,
    scaled_ref,
):
    step = pl.program_id(0)
    slots, nodes = adj_ref.shape
    layers = rhs_ref.shape[0]
    own_steps = nodes // SLOT_ROWS
    contract = (((1,), (1,)), ((), ()))

    @pl.when(step == 0)
    def _():
        for k in range(slots):
            same = coef_ref[k : k + 1, :]
            for m in range(slots):
                if m != k:
                    equal = adj_ref[k : k + 1, :] == adj_ref[m : m + 1, :]
                    same = same + jnp.where(equal, coef_ref[m : m + 1, :], 0.0)
            merged_ref[k : k + 1, :] = same
        keep = 1.0 - jnp.sum(coef_ref[...], axis=0, keepdims=True)
        rhs_ref[...] = thermal_ref[...] * keep
        for tile in range(nodes // NODE_TILE):
            cols = pl.ds(tile * NODE_TILE, NODE_TILE)
            merged = [merged_ref[k : k + 1, cols] for k in range(slots)]
            scale = best_scale(merged, 64)
            scale_ref[:, cols] = scale
            merged_ref[:, cols] = merged_ref[:, cols] / scale
            x = parts_ref[:layers, cols].astype(F32) + parts_ref[layers:, cols].astype(F32)
            x_high, x_low = halves(x * scale)
            scaled_ref[:layers, cols] = x_high
            scaled_ref[layers:, cols] = x_low

    here = pl.ds(pl.multiple_of(jnp.minimum(step, own_steps - 1) * SLOT_ROWS, SLOT_ROWS), SLOT_ROWS)
    high, low = halves(thermal_ref[:, here])
    is_own = step < own_steps
    high = jnp.where(is_own, high, received_ref[...])
    low = jnp.where(is_own, low, jnp.zeros_like(low))
    ext = jnp.concatenate([high, low], 0)
    row = lax.broadcasted_iota(jnp.int32, (SLOT_ROWS, NODE_TILE), 0).astype(F32).astype(BF16)
    total = jnp.zeros((2 * layers, SLOT_ROWS), F32)
    for tile in range(nodes // NODE_TILE):
        cols = pl.ds(tile * NODE_TILE, NODE_TILE)
        local = (adj_ref[:, cols] - step * SLOT_ROWS).astype(F32).astype(BF16)
        share = merged_ref[:, cols].astype(BF16)
        weights = jnp.zeros((SLOT_ROWS, NODE_TILE), BF16)
        for k in range(slots):
            weights = jnp.where(row == local[k : k + 1, :], share[k : k + 1, :], weights)
        part = jnp.dot(ext, weights, preferred_element_type=F32)
        rhs_ref[:, cols] += (part[:layers] + part[layers:]) * scale_ref[:, cols]
        total += lax.dot_general(
            scaled_ref[:, cols], weights, contract, preferred_element_type=F32
        )
    grad = total[:layers] + total[layers:]

    @pl.when(is_own)
    def _():
        keep = 1.0 - jnp.sum(coef_ref[:, here], axis=0, keepdims=True)
        whole_x = parts_ref[:layers, here].astype(F32) + parts_ref[layers:, here].astype(F32)
        own_ref[...] = whole_x * keep + grad

    @pl.when(jnp.logical_not(is_own))
    def _():
        halo_ref[...] = grad.T.astype(BF16)


def forcing_kernel(
    start_ref,
    factor_ref,
    window_ref,
    row_ref,
    col_ref,
    share_ref,
    surface_ref,
    thermal_ref,
    flux_ref,
    corr_ref,
    own_ref,
    left_ref,
    right_ref,
    grad_ref,
    *,
    band_width,
):
    fields, tile_rows, window_cols = grad_ref.shape
    half = left_ref.shape[1]
    tile = row_ref.shape[1]

    @pl.when(pl.program_id(0) == 0)
    def _():
        grad_ref[...] = jnp.zeros_like(grad_ref)

    share = share_ref[...]
    row_low = share[0:1] + share[2:3]
    row_high = share[1:2] + share[3:4]
    col_low = share[0:1] + share[1:2]
    col_high = share[2:3] + share[3:4]
    scale = best_scale([col_low, col_high], 64)
    col_low = col_low / scale
    col_high = col_high / scale
    base_row = row_ref[0:1, :]
    base_col = col_ref[0:1, :] - start_ref[0]
    base_col = jnp.where(base_col < 0, base_col + band_width, base_col)
    base_col = jnp.where(base_col >= band_width, base_col - band_width, base_col)
    row_at = lax.broadcasted_iota(jnp.int32, (tile_rows, tile), 0)
    col_at = lax.broadcasted_iota(jnp.int32, (window_cols, tile), 0)
    rows = jnp.where(
        row_at == base_row, row_low, jnp.where(row_at == base_row + 1, row_high, 0.0)
    )
    cols = jnp.where(
        col_at == base_col, col_low, jnp.where(col_at == base_col + 1, col_high, 0.0)
    )
    cols = cols.astype(BF16)
    window = window_ref[...].reshape(fields * tile_rows, window_cols)
    rows = rows * scale
    mixed = jnp.dot(window, cols, preferred_element_type=F32)
    forced = [
        jnp.sum(mixed[f * tile_rows : (f + 1) * tile_rows] * rows, axis=0, keepdims=True)
        for f in range(fields)
    ]
    wind = jnp.sqrt(forced[0] * forced[0] + forced[1] * forced[1] + 1.0)
    excess = forced[2] - thermal_ref[...]
    flux = 0.1 * wind * excess
    for f in range(fields):
        flux = flux + factor_ref[f] * forced[f]
    flux_ref[...] = flux
    surface = surface_ref[...]
    corr_ref[...] = -0.1 * surface * wind
    quotient = surface * (0.1 * excess / wind)
    dot = functools.partial(
        lax.dot_general,
        dimension_numbers=(((1,), (1,)), ((), ())),
        preferred_element_type=F32,
    )
    lefts = []
    for f in range(fields):
        node_grad = surface * factor_ref[f]
        if f < 2:
            node_grad = node_grad + quotient * forced[f]
        if f == 2:
            node_grad = node_grad + 0.1 * surface * wind
        lefts.append(halves(node_grad * rows))
    left_hi = jnp.concatenate([high for high, _ in lefts], 0)
    left_lo = jnp.concatenate([low for _, low in lefts], 0)
    grad = dot(left_hi, cols) + dot(left_lo, cols)
    grad_ref[...] += grad.reshape(fields, tile_rows, window_cols)

    @pl.when(pl.program_id(0) == pl.num_programs(0) - 1)
    def _():
        for f in range(fields):
            grad = grad_ref[f]
            left_ref[f] = grad[:, :half].T
            right_ref[f] = grad[:, window_cols - half :].T
            own_ref[f] = grad[:, half : window_cols - half]


def cost(flops, moved):
    return pl.CostEstimate(flops=flops, bytes_accessed=moved, transcendentals=0)


def per_device(
    atmosphere_inputs,
    thermal_anomaly,
    mixing_rates,
    adjacency_table,
    lateral_spread_factor,
    sent_vertices,
    corner_parallel,
    corner_longitude,
    corner_share,
    exchange_factor,
    sensitivity_vector,
):
    layers, nodes = thermal_anomaly.shape
    fields, tile_rows, tile_cols = atmosphere_inputs.shape
    half = tile_cols // 2
    columns = lax.axis_size("lon")
    halo = columns * sent_vertices.shape[1]
    slots = adjacency_table.shape[0]
    band_width = tile_cols * columns
    window_cols = 2 * tile_cols
    extended = nodes + halo
    params = pltpu.CompilerParams(vmem_limit_bytes=VMEM_BYTES)
    upward = [(i, (i + 1) % columns) for i in range(columns)]
    downward = [((i + 1) % columns, i) for i in range(columns)]
    start = (lax.axis_index("lon") * tile_cols - half).astype(jnp.int32).reshape(1)

    from_left = lax.ppermute(atmosphere_inputs[:, :, tile_cols - half :], "lon", upward)
    from_right = lax.ppermute(atmosphere_inputs[:, :, :half], "lon", downward)

    node_at = lax.broadcasted_iota(jnp.int32, (halo, nodes), 1)
    chosen = (sent_vertices.reshape(halo, 1) == node_at).astype(BF16)
    departing = lax.dot_general(
        chosen,
        thermal_anomaly.astype(BF16),
        (((1,), (1,)), ((), ())),
        preferred_element_type=F32,
    ).astype(BF16)
    received = lax.all_to_all(
        departing.reshape(columns, halo // columns, layers),
        "lon",
        split_axis=0,
        concat_axis=0,
        tiled=True,
    ).reshape(halo, layers)

    dense = (layers, nodes // LANES, LANES)
    block = jax.ShapeDtypeStruct(dense, F32)
    parts, surface, gain, scale, carry = pl.pallas_call(
        adjoint_kernel,
        out_shape=(
            jax.ShapeDtypeStruct((2 * layers, nodes), BF16),
            jax.ShapeDtypeStruct((1, nodes), F32),
            block,
            block,
            block,
        ),
        in_specs=whole(2),
        out_specs=tuple(whole(5)),
        scratch_shapes=[pltpu.VMEM(dense, F32), pltpu.VMEM(dense, F32)],
        compiler_params=params,
        cost_estimate=cost(layers * nodes * 20, layers * nodes * 24),
        name="adjoint_solve",
    )(mixing_rates, sensitivity_vector)

    own_steps = nodes // SLOT_ROWS
    rhs, own_grad, halo_grad = pl.pallas_call(
        lateral_kernel,
        grid=(extended // SLOT_ROWS,),
        out_shape=(
            jax.ShapeDtypeStruct((layers, nodes), F32),
            jax.ShapeDtypeStruct((layers, nodes), F32),
            jax.ShapeDtypeStruct((halo, layers), BF16),
        ),
        in_specs=[
            pl.BlockSpec((slots, nodes), lambda i: (0, 0)),
            pl.BlockSpec((slots, nodes), lambda i: (0, 0)),
            pl.BlockSpec((layers, nodes), lambda i: (0, 0)),
            pl.BlockSpec((layers, SLOT_ROWS), lambda i: (0, jnp.maximum(i - own_steps, 0))),
            pl.BlockSpec((2 * layers, nodes), lambda i: (0, 0)),
        ],
        out_specs=(
            pl.BlockSpec((layers, nodes), lambda i: (0, 0)),
            pl.BlockSpec((layers, SLOT_ROWS), lambda i: (0, jnp.minimum(i, own_steps - 1))),
            pl.BlockSpec((SLOT_ROWS, layers), lambda i: (jnp.maximum(i - own_steps, 0), 0)),
        ),
        scratch_shapes=[
            pltpu.VMEM((slots, nodes), F32),
            pltpu.VMEM((1, nodes), F32),
            pltpu.VMEM((2 * layers, nodes), BF16),
        ],
        compiler_params=params,
        cost_estimate=cost(8 * layers * nodes * extended, 8000000),
        name="lateral",
    )(
        adjacency_table,
        lateral_spread_factor,
        thermal_anomaly,
        received.T,
        parts,
    )
    back = lax.all_to_all(
        halo_grad.reshape(columns, halo // columns, layers),
        "lon",
        split_axis=0,
        concat_axis=0,
        tiled=True,
    ).reshape(halo, layers)

    window = jnp.concatenate([from_left, atmosphere_inputs, from_right], 2)
    line = pl.BlockSpec((1, FORCE_TILE), lambda i: (0, i))
    four = pl.BlockSpec((4, FORCE_TILE), lambda i: (0, i))

    def all_of(width):
        return pl.BlockSpec((fields, tile_rows, width), lambda i: (0, 0, 0))

    rim = pl.BlockSpec((fields, half, tile_rows), lambda i: (0, 0, 0))

    def grid_shape(width):
        return jax.ShapeDtypeStruct((fields, tile_rows, width), F32)

    flux, corr, own_forcing, left_rim, right_rim = pl.pallas_call(
        functools.partial(forcing_kernel, band_width=band_width),
        grid=(nodes // FORCE_TILE,),
        out_shape=(
            jax.ShapeDtypeStruct((1, nodes), F32),
            jax.ShapeDtypeStruct((1, nodes), F32),
            grid_shape(tile_cols),
            jax.ShapeDtypeStruct((fields, half, tile_rows), F32),
            jax.ShapeDtypeStruct((fields, half, tile_rows), F32),
        ),
        in_specs=[
            pl.BlockSpec(memory_space=pltpu.SMEM),
            pl.BlockSpec(memory_space=pltpu.SMEM),
            all_of(window_cols),
            four,
            four,
            four,
            line,
            line,
        ],
        out_specs=(line, line, all_of(tile_cols)) + (rim,) * 2,
        scratch_shapes=[pltpu.VMEM((fields, tile_rows, window_cols), F32)],
        compiler_params=params,
        cost_estimate=cost(8 * fields * tile_rows * window_cols * nodes, 4000000),
        name="forcing",
    )(
        start,
        exchange_factor,
        window,
        corner_parallel,
        corner_longitude,
        corner_share,
        surface,
        thermal_anomaly[0:1],
    )
    rim_from_left = lax.ppermute(right_rim, "lon", upward)
    rim_from_right = lax.ppermute(left_rim, "lon", downward)

    updated_warmth = pl.pallas_call(
        forward_kernel,
        out_shape=jax.ShapeDtypeStruct((layers, nodes), F32),
        in_specs=whole(5),
        out_specs=pl.BlockSpec(memory_space=pltpu.VMEM),
        scratch_shapes=[pltpu.VMEM(dense, F32)],
        compiler_params=params,
        cost_estimate=cost(layers * nodes * 6, layers * nodes * 20),
        name="forward_solve",
    )(rhs, flux, gain, scale, carry)

    returned = lax.dot_general(
        back, chosen, (((0,), (0,)), ((), ())), preferred_element_type=F32
    )
    top = lax.broadcasted_iota(jnp.int32, (layers, nodes), 0) == 0
    temp_grad = own_grad + jnp.where(top, corr, 0.0) + returned
    rims = jnp.concatenate([rim_from_left, rim_from_right], 1)
    forcing_grad = own_forcing + rims.transpose(0, 2, 1)
    return (updated_warmth, temp_grad, forcing_grad)


def solution(mesh):
    nodes = P(None, ("lat", "lon"))
    placed = (
        P(None, "lat", "lon"),
        nodes,
        nodes,
        nodes,
        nodes,
        P(("lat", "lon"), None),
        nodes,
        nodes,
        nodes,
        P(),
        nodes,
    )
    return jax.shard_map(
        per_device,
        mesh=mesh,
        in_specs=placed,
        out_specs=(nodes, nodes, P(None, "lat", "lon")),
        check_vma=False,
    )
```
